256 devices in a mesh: tm: 32 (over y, z), row: 8 (over x, core).
Axes of the slice: x: 4, y: 4, z: 8, core: 2. Of those that a mesh axis runs over, the one named last changes fastest.
Arguments:
- movie: float32 [2, 128, 1024, 1024], P(None, 'tm', 'row'), may hold values from -80 to 80, as said below
- cycle_label: int32 [1024, 1024], P(None, 'row'), may hold values from 0 to 127, as said below
- valid_mask: int32 [1024, 1024], P(None, 'row'), may hold values from 0 to 1, as said below
Outputs:
- cycle_curve: float32 [4, 128], replicated
- image_structure: float32 [4, 1024, 1024], P(None, 'tm', 'row')
The draws below stay inside these ranges and needn't reach their ends.
Inputs may be any that keep to these rules, and one draw needn't show every extreme that they name: `movie`: field components. `cycle_label`: cycle number of each frequency pixel; both 0 and 127 occur. `valid_mask`: some cycles have no counted pixel.
All inputs are finite; a program needn't handle non-finite values.
Results may differ from the reference program's by a relative error of at most 0.00023.
Values sent between devices are 32-bit elements; how exact they have to be, the bound alone decides.
No kernel may reach another device: no remote copies, remote signals or barrier semaphores. Data moves between devices by JAX's collectives and lax.ppermute only.
A program may use at most 128 MiB of HBM per device.

```python
import math
import jax
import jax.numpy as jnp
from jax import lax

N = 1024
LAGS = 4
CYCLES = 128
FRAMES = 128


smooth_weights = (1.0, 0.8, 0.6, 0.5, 0.4, 0.3, 0.2, 0.1)


def one_component(key, component):
    noise_key = jax.random.fold_in(key, 5 + 100 * component)
    static_key = jax.random.fold_in(key, 7 + 100 * component)
    extended = FRAMES + len(smooth_weights) - 1
    noise = jnp.clip(jax.random.normal(noise_key, (extended, N, N), jnp.float32), -6.0, 6.0)
    static = 1.0 + 0.5 * jnp.clip(jax.random.normal(static_key, (N, N), jnp.float32), -6.0, 6.0)
    rising = 2.0
    scale_total = math.sqrt(sum([weight * weight for weight in smooth_weights]))
    pattern = jnp.zeros((FRAMES, N, N), jnp.float32)
    for offset, weight in enumerate(smooth_weights):
        pattern = pattern + weight / scale_total * noise[offset:offset + FRAMES]
    times = jnp.arange(FRAMES, dtype=jnp.float32)
    growth = 1.0 + rising * times / (FRAMES - 1)
    return growth[:, None, None] * (static[None, :, :] + pattern)


def draw_movie(key, part):
    real_field = one_component(key, 0)
    imag_field = one_component(key, 1)
    return jnp.stack([real_field, imag_field]).astype(jnp.float32)


def cycle_layout(key):
    coeff_key = jax.random.fold_in(key, 11)
    scales = jax.random.randint(coeff_key, (2,), 32, 41)
    indices = jnp.arange(N, dtype=jnp.int32)
    folded = jnp.minimum(indices, N - indices)
    radius_sq = scales[0] * folded[:, None] * folded[:, None] + scales[1] * folded[None, :] * folded[None, :]
    cycle_unit = 64 * (N // 2) * (N // 2) // (CYCLES * CYCLES)

    def count_cycle(cycle_index, running):
        return running + (radius_sq >= cycle_unit * cycle_index * cycle_index).astype(jnp.int32)
    return lax.fori_loop(1, CYCLES, count_cycle, jnp.zeros((N, N), jnp.int32))


def draw_cycle_label(key, part):
    return cycle_layout(key)


def draw_valid_mask(key, part):
    labels = cycle_layout(key)
    mask_key = jax.random.fold_in(key, 23)
    cut_key, band_key, width_key, dead_key = jax.random.split(mask_key, 4)
    cutoff = jax.random.randint(cut_key, (), 1, 4)
    band_width = jax.random.randint(width_key, (), N // 16, N // 8 + 1)
    band_start = jax.random.randint(band_key, (), 0, N - N // 8)
    rows = jnp.arange(N, dtype=jnp.int32)[:, None]
    outside_band = (rows < band_start) | (rows >= band_start + band_width)
    alive = jax.random.randint(dead_key, (N, N), 0, 8) != 0
    return ((labels >= cutoff) & outside_band & alive).astype(jnp.int32)


def setup_inputs(seed: int = 0) -> dict:
    keys = jax.random.split(jax.random.key(seed), 4)
    return {
        "movie": draw_movie(jax.random.fold_in(keys[3], 71), 0),
        "cycle_label": draw_cycle_label(jax.random.fold_in(keys[3], 71), 0),
        "valid_mask": draw_valid_mask(jax.random.fold_in(keys[3], 71), 0),
    }


def reference(movie, cycle_label, valid_mask):
    field = movie[0] + 1j * movie[1]
    spectra = jnp.fft.fft2(field, norm="ortho")
    real_part = jnp.real(spectra)
    imag_part = jnp.imag(spectra)
    images = []
    for lag_value in range(1, LAGS + 1):
        diff_re = real_part[lag_value:] - real_part[:-lag_value]
        diff_im = imag_part[lag_value:] - imag_part[:-lag_value]
        summed = jnp.sum(diff_re * diff_re + diff_im * diff_im, axis=0)
        images.append(summed / (FRAMES - lag_value))
    image_structure = jnp.stack(images)
    weights = valid_mask.astype(jnp.float32).reshape(-1)
    labels = cycle_label.reshape(-1).astype(jnp.int32)
    flat_image = image_structure.reshape(LAGS, N * N)
    cycle_sum = jax.ops.segment_sum((flat_image * weights[None, :]).T, labels, num_segments=CYCLES)
    cycle_count = jax.ops.segment_sum(weights, labels, num_segments=CYCLES)
    cycle_curve = cycle_sum.T / jnp.maximum(cycle_count, 1.0)[None, :]
    return cycle_curve, image_structure
```

```python
import functools
import math

import jax
import jax.numpy as jnp
import ml_dtypes
import numpy as np
from jax import lax
from jax.experimental import pallas as pl
from jax.experimental.pallas import tpu as pltpu
from jax.sharding import Mesh
from jax.sharding import PartitionSpec as P

N = 1024
LAGS = 4
CYCLES = 128
FRAMES = 128
RADIX = 4
SUB = N // RADIX
OWN = 4
CHUNKS = ((0,), (1,), (2,), (3,))
ROW = ("row_0", "row_1")
TM = ("tm_0", "tm_1")

highest = lax.Precision.HIGHEST
f32 = jnp.float32
bf16 = jnp.bfloat16


def dft_tables():
    freq = 4 * np.arange(SUB)[None, :, None] + np.arange(RADIX)[:, None, None]
    phase = (freq * np.arange(SUB)[None, None, :]) % N
    angle = phase * (2.0 * math.pi / N)
    table = np.concatenate([np.cos(angle), np.sin(angle)], axis=2) / 32.0
    high = table.astype(ml_dtypes.bfloat16)
    low = (table - high.astype(np.float64)).astype(ml_dtypes.bfloat16)
    return high, low


def butterfly(parts_re, parts_im, p):
    (a, b, c, d), (e, f, g, h) = parts_re, parts_im
    if p == 0:
        return (a + c) + (b + d), (e + g) + (f + h)
    if p == 2:
        return (a + c) - (b + d), (e + g) - (f + h)
    if p == 1:
        return (a - c) + (f - h), (e - g) - (b - d)
    return (a - c) - (f - h), (e - g) + (b - d)


def split(z):
    high = z.astype(bf16)
    return high, (z - high.astype(f32)).astype(bf16)


def stacked(zr, zi):
    return jnp.concatenate(
        [jnp.concatenate([zr, zi], axis=1), jnp.concatenate([zi, -zr], axis=1)], axis=0
    )


def nt(a, b):
    return lax.dot_general(a, b, (((1,), (1,)), ((), ())), preferred_element_type=f32)


def first_kernel(residues, movie_ref, high_ref, low_ref, out_ref):
    parts = [[movie_ref[c, 0, :, q * SUB:(q + 1) * SUB] for q in range(RADIX)] for c in range(2)]
    for j, p in enumerate(residues):
        zr, zi = butterfly(parts[0], parts[1], p)
        zh, zl = split(stacked(zr, zi))
        th, tl = high_ref[j], low_ref[j]
        got = nt(th, zh) + nt(tl, zh) + nt(th, zl)
        rows = got.shape[1] // 2
        for c in range(2):
            piece = got[:, c * rows:(c + 1) * rows]
            out_ref[:, c, j] = piece.reshape(out_ref.shape[0], 32, rows)


def first_transform(movie, high, low, index, residues):
    count = len(residues)
    return pl.pallas_call(
        functools.partial(first_kernel, residues),
        grid=(OWN,),
        in_specs=[
            pl.BlockSpec((2, 1, 128, N), lambda f: (0, f, 0, 0)),
            pl.BlockSpec((count, SUB, 2 * SUB), lambda f: (index, 0, 0)),
            pl.BlockSpec((count, SUB, 2 * SUB), lambda f: (index, 0, 0)),
        ],
        out_specs=pl.BlockSpec((8, 2, count, 32, 128), lambda f: (0, 0, 0, 0, f)),
        out_shape=jax.ShapeDtypeStruct((8, 2, count, 32, OWN * 128), f32),
        compiler_params=pltpu.CompilerParams(vmem_limit_bytes=24 << 20),
        cost_estimate=pl.CostEstimate(
            flops=count * 6 * 256 * 512 * 1024, bytes_accessed=(4 + count) << 20, transcendentals=0
        ),
        name="first_transform",
    )(movie, high, low)


def second_kernel(count, piece_ref, high_ref, low_ref, early_ref, late_ref):
    for j in range(count):

        def part(c, q):
            halves = []
            for h in range(2):
                s = 2 * q + h
                halves.append(
                    jnp.concatenate(
                        [piece_ref[s, c, j, :, f * 128:(f + 1) * 128] for f in range(OWN)], axis=0
                    )
                )
            return jnp.concatenate(halves, axis=1)

        parts = [[part(c, q) for q in range(RADIX)] for c in range(2)]
        for p in range(RADIX):
            zr, zi = butterfly(parts[0], parts[1], p)
            zh, zl = split(stacked(zr, zi))
            th, tl = high_ref[p], low_ref[p]
            got = nt(zh, th) + nt(zh, tl) + nt(zl, th)
            for c in range(2):
                for f in range(OWN):
                    ref = early_ref if f < 2 else late_ref
                    ref[f % 2, c, j, :, p * SUB:(p + 1) * SUB] = got[
                        (c * OWN + f) * 32:(c * OWN + f + 1) * 32
                    ]


def second_transform(piece, high, low, count):
    half = jax.ShapeDtypeStruct((2, 2, count, 32, N), f32)
    return pl.pallas_call(
        functools.partial(second_kernel, count),
        out_shape=(half, half),
        compiler_params=pltpu.CompilerParams(vmem_limit_bytes=40 << 20),
        cost_estimate=pl.CostEstimate(
            flops=count * 6 * 256 * 512 * 1024, bytes_accessed=(2 + 2 * count) << 20, transcendentals=0
        ),
        name="second_transform",
    )(piece, high, low)


def lag_kernel(count, ends_ref, early_ref, late_ref, right_ref, left_ref, out_ref):
    has_right, has_left = ends_ref[0], ends_ref[1]
    for j in range(count):
        for b in range(8):
            lanes = slice(b * 128, (b + 1) * 128)
            frames = {}
            for f in range(2):
                frames[f] = [early_ref[f, c, j, :, lanes] for c in range(2)]
                frames[2 + f] = [late_ref[f, c, j, :, lanes] for c in range(2)]
                frames[4 + f] = [right_ref[f, c, j, :, lanes] for c in range(2)]
                frames[f - 2] = [left_ref[f, c, j, :, lanes] for c in range(2)]

            def pair(s, t):
                dr = frames[t][0] - frames[s][0]
                di = frames[t][1] - frames[s][1]
                return dr * dr + di * di

            def total(pairs):
                return functools.reduce(lambda x, y: x + y, [pair(s, t) for s, t in pairs])

            lag_rows = []
            for lag in range(1, LAGS + 1):
                own = [(s, s + lag) for s in range(OWN) if s + lag < OWN]
                right = [(s, s + lag) for s in range(OWN) if 4 <= s + lag < 6]
                left = [(s, s + lag) for s in (-2, -1) if s + lag in (2, 3)]
                terms = []
                if own:
                    terms.append(total(own))
                terms.append(has_right * total(right))
                if left:
                    terms.append(has_left * total(left))
                whole = functools.reduce(lambda x, y: x + y, terms)
                lag_rows.append(whole * (1.0 / float(FRAMES - lag)))
            block = jnp.concatenate(lag_rows, axis=0).T
            p, h = b // 2, b % 2
            out_ref[2 * h:2 * h + 2, :, j, p] = block.reshape(2, 8, 8, 128)


def partial_lags(ends, early, late, right, left, count):
    vmem = pl.BlockSpec(memory_space=pltpu.VMEM)
    return pl.pallas_call(
        functools.partial(lag_kernel, count),
        in_specs=[pl.BlockSpec(memory_space=pltpu.SMEM)] + [vmem] * 4,
        out_specs=vmem,
        out_shape=jax.ShapeDtypeStruct((4, 8, count, RADIX, 8, 128), f32),
        compiler_params=pltpu.CompilerParams(vmem_limit_bytes=24 << 20),
        cost_estimate=pl.CostEstimate(
            flops=count * 100 * 32 * 1024, bytes_accessed=count * 5 << 19, transcendentals=0
        ),
        name="partial_lags",
    )(ends, early, late, right, left)


def cycle_table(labels, mask_block, cycle_count):
    cycle_ids = jnp.arange(cycle_count, dtype=jnp.int32)
    chosen = (labels.reshape(-1)[:, None] == cycle_ids[None, :]) & (
        mask_block.reshape(-1)[:, None] == 1
    )
    return chosen.astype(f32)


def sum_everywhere(value):
    for axes in (ROW, TM):
        size = lax.axis_size(axes)
        copies = jnp.broadcast_to(value[None], (size,) + value.shape)
        value = jnp.sum(lax.all_to_all(copies, axes, 0, 0, tiled=True), axis=0)
    return value


def body(movie, cycle_label, valid_mask):
    high, low = dft_tables()
    high, low = jnp.asarray(high), jnp.asarray(low)
    time_count = lax.axis_size(TM)
    time_place = lax.axis_index(TM)
    slab_rows = N // time_count
    slab_labels = lax.dynamic_slice_in_dim(cycle_label, time_place * slab_rows, slab_rows, 0)
    slab_mask = lax.dynamic_slice_in_dim(valid_mask, time_place * slab_rows, slab_rows, 0)
    slab_table = cycle_table(slab_labels, slab_mask, CYCLES)
    counts = jnp.sum(slab_table, axis=0)
    ends = jnp.stack([time_place < time_count - 1, time_place > 0]).astype(f32)
    to_left = [(i + 1, i) for i in range(time_count - 1)]
    to_right = [(i, i + 1) for i in range(time_count - 1)]
    slabs = []
    for index, residues in enumerate(CHUNKS):
        count = len(residues)
        piece = first_transform(movie, high, low, index, residues)
        piece = lax.all_to_all(piece, ROW, 0, 0, tiled=True)
        early, late = second_transform(piece, high, low, count)
        right = lax.ppermute(early, TM, to_left)
        left = lax.ppermute(late, TM, to_right)
        part = partial_lags(ends, early, late, right, left, count)
        part = jnp.sum(lax.all_to_all(part, "tm_0", 0, 0, tiled=True), axis=0)
        part = jnp.sum(lax.all_to_all(part, "tm_1", 0, 0, tiled=True), axis=0)
        slabs.append(part)
    slab = jnp.concatenate(slabs, axis=0).reshape(RADIX, RADIX, 8, LAGS, 32)
    image_structure = jnp.transpose(slab, (3, 2, 1, 4, 0)).reshape(LAGS, slab_rows, 128)
    cycle_part = jnp.dot(
        image_structure.reshape(LAGS, -1), slab_table, precision=highest, preferred_element_type=f32
    )
    sums = sum_everywhere(jnp.concatenate([cycle_part, counts[None, :]], axis=0))
    cycle_curve = sums[:LAGS] / jnp.maximum(sums[LAGS], 1.0)[None, :]
    return (cycle_curve, image_structure)


def solution(mesh):
    torus = Mesh(mesh.devices.reshape(4, 8, 4, 2), ("tm_0", "tm_1", "row_0", "row_1"))
    placed = (P(None, TM, ROW, None), P(None, ROW), P(None, ROW))
    return jax.shard_map(
        body, mesh=torus, in_specs=placed, out_specs=(P(), P(None, TM, ROW)), check_vma=False
    )
```

```python
import functools
import math

import jax
import jax.numpy as jnp
import ml_dtypes
import numpy as np
from jax import lax
from jax.experimental import pallas as pl
from jax.experimental.pallas import tpu as pltpu
from jax.sharding import Mesh
from jax.sharding import PartitionSpec as P

N = 1024
LAGS = 4
CYCLES = 128
FRAMES = 128
RADIX = 4
SUB = N // RADIX
OWN = 4
CHUNKS = ((0, 1), (2,), (3,))
ROW = ("row_0", "row_1")
TM = ("tm_0", "tm_1")
YROW = ("tm_0", "row_0", "row_1")

f32 = jnp.float32
bf16 = jnp.bfloat16


def dft_tables():
    freq = 4 * np.arange(SUB)[None, :, None] + np.arange(RADIX)[:, None, None]
    phase = (freq * np.arange(SUB)[None, None, :]) % N
    angle = phase * (2.0 * math.pi / N)
    table = np.concatenate([np.cos(angle), np.sin(angle)], axis=2) / 32.0
    high = table.astype(ml_dtypes.bfloat16)
    low = (table - high.astype(np.float64)).astype(ml_dtypes.bfloat16)
    return high, low


def butterfly(parts_re, parts_im, p):
    (a, b, c, d), (e, f, g, h) = parts_re, parts_im
    if p == 0:
        return (a + c) + (b + d), (e + g) + (f + h)
    if p == 2:
        return (a + c) - (b + d), (e + g) - (f + h)
    if p == 1:
        return (a - c) + (f - h), (e - g) - (b - d)
    return (a - c) - (f - h), (e - g) + (b - d)


def split(z):
    high = z.astype(bf16)
    return high, (z - high.astype(f32)).astype(bf16)


def stacked(zr, zi):
    return jnp.concatenate(
        [jnp.concatenate([zr, zi], axis=1), jnp.concatenate([zi, -zr], axis=1)], axis=0
    )


def nt(a, b):
    return lax.dot_general(a, b, (((1,), (1,)), ((), ())), preferred_element_type=f32)


def first_kernel(residues, movie_ref, high_ref, low_ref, out_ref):
    parts = [[movie_ref[c, 0, :, q * SUB:(q + 1) * SUB] for q in range(RADIX)] for c in range(2)]
    for j, p in enumerate(residues):
        zr, zi = butterfly(parts[0], parts[1], p)
        zh, zl = split(stacked(zr, zi))
        th, tl = high_ref[p], low_ref[p]
        got = nt(th, zh) + nt(tl, zh) + nt(th, zl)
        for c in range(2):
            piece = got[:, c * 128:(c + 1) * 128].reshape(8, 4, 8, 128)
            for y in range(4):
                out_ref[y, :, c, j] = piece[:, y]


def first_transform(movie, high, low, residues):
    count = len(residues)
    table = pl.BlockSpec((RADIX, SUB, 2 * SUB), lambda f: (0, 0, 0))
    return pl.pallas_call(
        functools.partial(first_kernel, residues),
        grid=(OWN,),
        in_specs=[pl.BlockSpec((2, 1, 128, N), lambda f: (0, f, 0, 0)), table, table],
        out_specs=pl.BlockSpec((4, 8, 2, count, 8, 128), lambda f: (0, 0, 0, 0, 0, f)),
        out_shape=jax.ShapeDtypeStruct((4, 8, 2, count, 8, OWN * 128), f32),
        compiler_params=pltpu.CompilerParams(vmem_limit_bytes=24 << 20),
        cost_estimate=pl.CostEstimate(
            flops=count * 6 * 256 * 512 * 1024, bytes_accessed=(4 + count) << 20, transcendentals=0
        ),
        name="first_transform",
    )(movie, high, low)


def second_kernel(count, piece_ref, high_ref, low_ref, early_ref, late_ref):
    for j in range(count):

        def part(c, q):
            return jnp.concatenate(
                [
                    jnp.concatenate(
                        [
                            piece_ref[y, 2 * q + h, c, j, :, f * 128:(f + 1) * 128]
                            for f in range(OWN)
                            for y in range(4)
                        ],
                        axis=0,
                    )
                    for h in range(2)
                ],
                axis=1,
            )

        parts = [[part(c, q) for q in range(RADIX)] for c in range(2)]
        for p in range(RADIX):
            zr, zi = butterfly(parts[0], parts[1], p)
            zh, zl = split(stacked(zr, zi))
            th, tl = high_ref[p], low_ref[p]
            got = nt(zh, th) + nt(zh, tl) + nt(zl, th)
            for c in range(2):
                for f in range(OWN):
                    ref = early_ref if f < 2 else late_ref
                    ref[f % 2, c, j, :, p * SUB:(p + 1) * SUB] = got[
                        (c * OWN + f) * 32:(c * OWN + f + 1) * 32
                    ]


def second_transform(piece, high, low, count):
    half = jax.ShapeDtypeStruct((2, 2, count, 32, N), f32)
    return pl.pallas_call(
        functools.partial(second_kernel, count),
        out_shape=(half, half),
        compiler_params=pltpu.CompilerParams(vmem_limit_bytes=40 << 20),
        cost_estimate=pl.CostEstimate(
            flops=count * 6 * 256 * 512 * 1024, bytes_accessed=(2 + 2 * count) << 20, transcendentals=0
        ),
        name="second_transform",
    )(piece, high, low)


def lag_kernel(
    count, final, ends_ref, early_ref, late_ref, right_ref, left_ref, label_ref, before_ref,
    out_ref, cycle_ref, lags_ref
):
    at_end, at_start = ends_ref[0], ends_ref[1]
    has_right = 1.0 - at_end.astype(f32)
    has_left = 1.0 - at_start.astype(f32)
    cycle_row = lax.broadcasted_iota(jnp.int32, (CYCLES, SUB), 0)
    sub_row = lax.broadcasted_iota(jnp.int32, (32, CYCLES), 0) % 8
    ones = jnp.ones((16, SUB), bf16)
    cycle_sums = jnp.zeros((32, CYCLES), f32)
    cycle_counts = jnp.zeros((16, CYCLES), f32)
    for j in range(count):
        for b in range(8):
            lanes = slice(b * 128, (b + 1) * 128)
            sums = [0.0] * LAGS
            for y in range(4):
                own_rows = slice(y * 8, (y + 1) * 8)
                right_rows = pl.ds(pl.multiple_of(8 * jnp.minimum(y + at_end, 3), 8), 8)
                left_rows = pl.ds(pl.multiple_of(8 * jnp.maximum(y - at_start, 0), 8), 8)
                frames = {}
                for f in range(2):
                    frames[f] = [early_ref[f, c, j, own_rows, lanes] for c in range(2)]
                    frames[2 + f] = [late_ref[f, c, j, own_rows, lanes] for c in range(2)]
                    frames[4 + f] = [right_ref[f, c, j, right_rows, lanes] for c in range(2)]
                    frames[f - 2] = [left_ref[f, c, j, left_rows, lanes] for c in range(2)]

                def total(pairs):
                    terms = []
                    for s, t in pairs:
                        dr = frames[t][0] - frames[s][0]
                        di = frames[t][1] - frames[s][1]
                        terms.append(dr * dr + di * di)
                    return functools.reduce(lambda x, z: x + z, terms)

                for lag in range(1, LAGS + 1):
                    own = [(s, s + lag) for s in range(OWN) if s + lag < OWN]
                    right = [(s, s + lag) for s in range(OWN) if 4 <= s + lag < 6]
                    left = [(s, s + lag) for s in (-2, -1) if s + lag in (2, 3)]
                    terms = [sums[lag - 1]]
                    if own:
                        terms.append(total(own))
                    terms.append(total(right) * has_right if y == 3 else total(right))
                    if left:
                        terms.append(total(left) * has_left if y == 0 else total(left))
                    sums[lag - 1] = functools.reduce(lambda x, z: x + z, terms)
            p, h = b // 2, b % 2
            for lag in range(1, LAGS + 1):
                lags_ref[p * 32 + (lag - 1) * 8:p * 32 + lag * 8, h * 128:(h + 1) * 128] = sums[
                    lag - 1
                ] * (1.0 / float(FRAMES - lag))
        for h in range(2):
            block = lags_ref[:, h * 128:(h + 1) * 128].T
            out_ref[16 * h:16 * h + 16, j] = block.reshape(16, 8, 128)
        for p in range(RADIX):
            dh, dl = split(lags_ref[p * 32:(p + 1) * 32, :])
            rows = jnp.concatenate([dh, dl, ones], axis=0)
            for k in range(8):
                chosen = jnp.where(cycle_row == label_ref[j, p, k:k + 1, :], 1.0, 0.0).astype(bf16)
                got = nt(rows, chosen)
                cycle_sums += jnp.where(sub_row == k, got[:32] + got[32:64], 0.0)
                cycle_counts += got[64:]
    tile = jnp.concatenate(
        [
            jnp.sum(cycle_sums.reshape(LAGS, 8, CYCLES), axis=1),
            cycle_counts[:1] * 0.125,
            jnp.zeros((3, CYCLES), f32),
        ],
        axis=0,
    ) + before_ref[...]
    cycle_ref[...] = tile
    if final:
        for m in range(32):
            out_ref[m, count] = tile


def partial_lags(ends, early, late, right, left, labels, before, count, final):
    vmem = pl.BlockSpec(memory_space=pltpu.VMEM)
    return pl.pallas_call(
        functools.partial(lag_kernel, count, final),
        in_specs=[pl.BlockSpec(memory_space=pltpu.SMEM)] + [vmem] * 6,
        out_specs=(vmem, vmem),
        out_shape=(
            jax.ShapeDtypeStruct((32, count + int(final), 8, 128), f32),
            jax.ShapeDtypeStruct((8, CYCLES), f32),
        ),
        scratch_shapes=[pltpu.VMEM((128, SUB), f32)],
        compiler_params=pltpu.CompilerParams(vmem_limit_bytes=24 << 20),
        cost_estimate=pl.CostEstimate(
            flops=count * 64 * 80 * 256 * 128, bytes_accessed=count * 5 << 19, transcendentals=0
        ),
        name="partial_lags",
    )(ends, early, late, right, left, labels, before)


def body(movie, cycle_label, valid_mask):
    high, low = dft_tables()
    high, low = jnp.asarray(high), jnp.asarray(low)
    z_count = lax.axis_size("tm_1")
    z_place = lax.axis_index("tm_1")
    ends = jnp.stack([z_place == z_count - 1, z_place == 0]).astype(jnp.int32)
    labels = jnp.where(valid_mask == 1, cycle_label, -1)
    labels = lax.dynamic_slice_in_dim(labels, lax.axis_index("tm_0") * 32, 32, 1)
    labels = labels.reshape(SUB, RADIX, 8, RADIX).transpose(3, 1, 2, 0)
    to_left = [(i, (i - 1) % z_count) for i in range(z_count)]
    to_right = [(i, (i + 1) % z_count) for i in range(z_count)]
    cycles = jnp.zeros((8, CYCLES), f32)
    slabs = []
    done = []
    for index, residues in enumerate(CHUNKS):
        count = len(residues)
        final = index == len(CHUNKS) - 1
        piece = first_transform(movie, high, low, residues)
        if index >= 2:
            piece, done[index - 2] = lax.optimization_barrier((piece, done[index - 2]))
        piece = piece.reshape((32,) + piece.shape[2:])
        piece = lax.all_to_all(piece, YROW, 0, 0, tiled=True)
        piece = piece.reshape((4, 8) + piece.shape[1:])
        early, late = second_transform(piece, high, low, count)
        done.append((early, late))
    for index, residues in enumerate(CHUNKS):
        count = len(residues)
        final = index == len(CHUNKS) - 1
        early, late = done[index]
        right = lax.ppermute(early, "tm_1", to_left)
        left = lax.ppermute(late, "tm_1", to_right)
        part, cycles = partial_lags(
            ends, early, late, right, left, labels[residues[0]:residues[-1] + 1], cycles, count, final
        )
        part = lax.all_to_all(part, TM, 0, 0, tiled=True)
        if final:
            cycles = jnp.sum(part[:, count], axis=0)
        slabs.append(jnp.sum(part[:, :count].reshape(4, 8, count, 8, 128), axis=1))
    slab = jnp.concatenate(slabs, axis=1).reshape(4, RADIX, 8, RADIX, LAGS, 8)
    image_structure = jnp.transpose(slab, (4, 2, 3, 0, 5, 1)).reshape(LAGS, 32, 128)
    copies = jnp.broadcast_to(cycles[None], (8,) + cycles.shape)
    sums = jnp.sum(lax.all_to_all(copies, ROW, 0, 0, tiled=True), axis=0)
    cycle_curve = sums[:LAGS] / jnp.maximum(sums[LAGS], 1.0)[None, :]
    return (cycle_curve, image_structure)


def solution(mesh):
    torus = Mesh(mesh.devices.reshape(4, 8, 4, 2), ("tm_0", "tm_1", "row_0", "row_1"))
    placed = (P(None, TM, ROW, None), P(None, ROW), P(None, ROW))
    return jax.shard_map(
        body, mesh=torus, in_specs=placed, out_specs=(P(), P(None, TM, ROW)), check_vma=False
    )
```

```python
import functools
import math

import jax
import jax.numpy as jnp
import ml_dtypes
import numpy as np
from jax import lax
from jax.experimental import pallas as pl
from jax.experimental.pallas import tpu as pltpu
from jax.sharding import Mesh
from jax.sharding import PartitionSpec as P

N = 1024
LAGS = 4
CYCLES = 128
FRAMES = 128
RADIX = 4
SUB = N // RADIX
OWN = 4
REST_VMEM, SECOND_VMEM, LAG_VMEM = 56, 24, 24
CHUNKS = ((0, 1), (2,), (3,))
ROW = ("row_0", "row_1")
TM = ("tm_0", "tm_1")
YROW = ("tm_0", "row_0", "row_1")

f32 = jnp.float32
bf16 = jnp.bfloat16


def dft_tables():
    freq = 4 * np.arange(SUB)[None, :, None] + np.arange(RADIX)[:, None, None]
    phase = (freq * np.arange(SUB)[None, None, :]) % N
    angle = phase * (2.0 * math.pi / N)
    table = np.concatenate([np.cos(angle), np.sin(angle)], axis=2) / 32.0
    high = table.astype(ml_dtypes.bfloat16)
    low = (table - high.astype(np.float64)).astype(ml_dtypes.bfloat16)
    return high, low


def butterfly(parts_re, parts_im, p):
    (a, b, c, d), (e, f, g, h) = parts_re, parts_im
    if p == 0:
        return (a + c) + (b + d), (e + g) + (f + h)
    if p == 2:
        return (a + c) - (b + d), (e + g) - (f + h)
    if p == 1:
        return (a - c) + (f - h), (e - g) - (b - d)
    return (a - c) - (f - h), (e - g) + (b - d)


def split(z):
    high = z.astype(bf16)
    return high, (z - high.astype(f32)).astype(bf16)


def stacked(zr, zi):
    return jnp.concatenate(
        [jnp.concatenate([zr, zi], axis=1), jnp.concatenate([zi, -zr], axis=1)], axis=0
    )


def nt(a, b):
    return lax.dot_general(a, b, (((1,), (1,)), ((), ())), preferred_element_type=f32)


def first_kernel(residues, movie_ref, high_ref, low_ref, *refs):
    out_ref = refs[-1]
    parts = [[movie_ref[c, 0, :, q * SUB:(q + 1) * SUB] for q in range(RADIX)] for c in range(2)]
    for j, p in enumerate(residues):
        zr, zi = butterfly(parts[0], parts[1], p)
        zh, zl = split(stacked(zr, zi))
        th, tl = high_ref[j], low_ref[j]
        got = nt(th, zh) + nt(tl, zh) + nt(th, zl)
        for c in range(2):
            piece = got[:, c * 128:(c + 1) * 128].reshape(8, 4, 8, 128)
            for y in range(4):
                out_ref[y, :, c, j] = piece[:, y]


def first_transform(movie, high, low, residues, after):
    count = len(residues)
    place = residues[0] // count
    table = pl.BlockSpec((count, SUB, 2 * SUB), lambda f: (place, 0, 0))
    order = [pl.BlockSpec(memory_space=pl.ANY)] * len(after)
    return pl.pallas_call(
        functools.partial(first_kernel, residues),
        grid=(OWN,),
        in_specs=[pl.BlockSpec((2, 1, 128, N), lambda f: (0, f, 0, 0)), table, table] + order,
        out_specs=pl.BlockSpec((4, 8, 2, count, 8, 128), lambda f: (0, 0, 0, 0, 0, f)),
        out_shape=jax.ShapeDtypeStruct((4, 8, 2, count, 8, OWN * 128), f32),
        compiler_params=pltpu.CompilerParams(vmem_limit_bytes=(56 if residues[0] == 0 else REST_VMEM) << 20),
        cost_estimate=pl.CostEstimate(
            flops=1024, bytes_accessed=1024, transcendentals=0
        ),
        name="first_transform",
    )(movie, high, low, *after)


def second_kernel(count, piece_ref, high_ref, low_ref, *refs):
    early_ref, late_ref, token_ref = refs[-3:]
    token_ref[...] = jnp.zeros_like(token_ref)
    for j in range(count):

        def part(c, q):
            return jnp.concatenate(
                [
                    jnp.concatenate(
                        [
                            piece_ref[y, 2 * q + h, c, j, :, f * 128:(f + 1) * 128]
                            for f in range(OWN)
                            for y in range(4)
                        ],
                        axis=0,
                    )
                    for h in range(2)
                ],
                axis=1,
            )

        parts = [[part(c, q) for q in range(RADIX)] for c in range(2)]
        for p in range(RADIX):
            zr, zi = butterfly(parts[0], parts[1], p)
            zh, zl = split(stacked(zr, zi))
            th, tl = high_ref[p], low_ref[p]
            got = nt(zh, th) + nt(zh, tl) + nt(zl, th)
            for c in range(2):
                for f in range(OWN):
                    ref = early_ref if f < 2 else late_ref
                    ref[f % 2, c, j, :, p * SUB:(p + 1) * SUB] = got[
                        (c * OWN + f) * 32:(c * OWN + f + 1) * 32
                    ]


def second_transform(piece, high, low, count, after):
    vmem = pl.BlockSpec(memory_space=pltpu.VMEM)
    half = jax.ShapeDtypeStruct((2, 2, count, 32, N), f32)
    return pl.pallas_call(
        functools.partial(second_kernel, count),
        in_specs=[vmem] * 3 + [pl.BlockSpec(memory_space=pl.ANY)] * len(after),
        out_shape=(half, half, jax.ShapeDtypeStruct((8, 128), f32)),
        compiler_params=pltpu.CompilerParams(vmem_limit_bytes=SECOND_VMEM << 20),
        cost_estimate=pl.CostEstimate(
            flops=1024, bytes_accessed=1024, transcendentals=0
        ),
        name="second_transform",
    )(piece, high, low, *after)


def lag_kernel(
    count, carried, final, ends_ref, early_ref, late_ref, right_ref, left_ref, label_ref, before_ref,
    *refs
):
    out_ref, cycle_ref, lags_ref = refs[-3:]
    if carried:
        out_ref[:, count:count + carried] = refs[0][...]
    at_end, at_start = ends_ref[0], ends_ref[1]
    has_right = 1.0 - at_end.astype(f32)
    has_left = 1.0 - at_start.astype(f32)
    cycle_row = lax.broadcasted_iota(jnp.int32, (CYCLES, SUB), 0)
    sub_row = lax.broadcasted_iota(jnp.int32, (32, CYCLES), 0) % 8
    ones = jnp.ones((16, SUB), bf16)
    cycle_sums = jnp.zeros((32, CYCLES), f32)
    cycle_counts = jnp.zeros((16, CYCLES), f32)
    for j in range(count):
        for b in range(8):
            lanes = slice(b * 128, (b + 1) * 128)
            sums = [0.0] * LAGS
            for y in range(4):
                own_rows = slice(y * 8, (y + 1) * 8)
                right_rows = pl.ds(pl.multiple_of(8 * jnp.minimum(y + at_end, 3), 8), 8)
                left_rows = pl.ds(pl.multiple_of(8 * jnp.maximum(y - at_start, 0), 8), 8)
                frames = {}
                for f in range(2):
                    frames[f] = [early_ref[f, c, j, own_rows, lanes] for c in range(2)]
                    frames[2 + f] = [late_ref[f, c, j, own_rows, lanes] for c in range(2)]
                    frames[4 + f] = [right_ref[f, c, j, right_rows, lanes] for c in range(2)]
                    frames[f - 2] = [left_ref[f, c, j, left_rows, lanes] for c in range(2)]

                def total(pairs):
                    terms = []
                    for s, t in pairs:
                        dr = frames[t][0] - frames[s][0]
                        di = frames[t][1] - frames[s][1]
                        terms.append(dr * dr + di * di)
                    return functools.reduce(lambda x, z: x + z, terms)

                for lag in range(1, LAGS + 1):
                    own = [(s, s + lag) for s in range(OWN) if s + lag < OWN]
                    right = [(s, s + lag) for s in range(OWN) if 4 <= s + lag < 6]
                    left = [(s, s + lag) for s in (-2, -1) if s + lag in (2, 3)]
                    terms = [sums[lag - 1]]
                    if own:
                        terms.append(total(own))
                    terms.append(total(right) * has_right if y == 3 else total(right))
                    if left:
                        terms.append(total(left) * has_left if y == 0 else total(left))
                    sums[lag - 1] = functools.reduce(lambda x, z: x + z, terms)
            p, h = b // 2, b % 2
            for lag in range(1, LAGS + 1):
                lags_ref[p * 32 + (lag - 1) * 8:p * 32 + lag * 8, h * 128:(h + 1) * 128] = sums[
                    lag - 1
                ] * (1.0 / float(FRAMES - lag))
        for h in range(2):
            block = lags_ref[:, h * 128:(h + 1) * 128].T
            out_ref[16 * h:16 * h + 16, j] = block.reshape(16, 8, 128)
        for p in range(RADIX):
            dh, dl = split(lags_ref[p * 32:(p + 1) * 32, :])
            rows = jnp.concatenate([dh, dl, ones], axis=0)
            for k in range(8):
                chosen = jnp.where(cycle_row == label_ref[j, p, k:k + 1, :], 1.0, 0.0).astype(bf16)
                got = nt(rows, chosen)
                cycle_sums += jnp.where(sub_row == k, got[:32] + got[32:64], 0.0)
                cycle_counts += got[64:]
    tile = jnp.concatenate(
        [
            jnp.sum(cycle_sums.reshape(LAGS, 8, CYCLES), axis=1),
            cycle_counts[:1] * 0.125,
            jnp.zeros((3, CYCLES), f32),
        ],
        axis=0,
    ) + before_ref[...]
    cycle_ref[...] = tile
    if final:
        for m in range(32):
            out_ref[m, count + carried] = tile


def partial_lags(ends, early, late, right, left, labels, before, carry, after, final):
    count = early.shape[2]
    carried = sum(c.shape[1] for c in carry)
    vmem = pl.BlockSpec(memory_space=pltpu.VMEM)
    return pl.pallas_call(
        functools.partial(lag_kernel, count, carried, final),
        in_specs=[pl.BlockSpec(memory_space=pltpu.SMEM)]
        + [vmem] * (6 + len(carry))
        + [pl.BlockSpec(memory_space=pl.ANY)] * len(after),
        out_specs=(vmem, vmem),
        out_shape=(
            jax.ShapeDtypeStruct((32, count + carried + int(final), 8, 128), f32),
            jax.ShapeDtypeStruct((8, CYCLES), f32),
        ),
        scratch_shapes=[pltpu.VMEM((128, SUB), f32)],
        compiler_params=pltpu.CompilerParams(vmem_limit_bytes=LAG_VMEM << 20),
        cost_estimate=pl.CostEstimate(
            flops=1024, bytes_accessed=1024, transcendentals=0
        ),
        name="partial_lags",
    )(ends, early, late, right, left, labels, before, *carry, *after)


def settle_kernel(places, *refs):
    out_ref = refs[-1]
    lane = lax.broadcasted_iota(jnp.int32, (8, 128), 1)
    from_lane = (lane % 32) // 4
    tiles = []
    for y in range(4):
        for p in range(RADIX):
            which, j = places[p]
            tile = refs[which][8 * y, j]
            for z in range(1, 8):
                tile = tile + refs[which][8 * y + z, j]
            tiles.append((tile, (lane // 32 == y) & (lane % 4 == p)))
    for q in range(RADIX):
        for lag in range(LAGS):
            index = from_lane + (q * 32 + lag * 8)
            out = jnp.zeros((8, 128), f32)
            for tile, here in tiles:
                out = jnp.where(here, jnp.take_along_axis(tile, index, axis=1), out)
            out_ref[lag, pl.ds(q, 8, stride=4), :] = out


def settle(sums_0, sums_1):
    places = {}
    for j, p in enumerate(CHUNKS[0]):
        places[p] = (0, j)
    for j, p in enumerate(CHUNKS[2] + CHUNKS[1]):
        places[p] = (1, j)
    return pl.pallas_call(
        functools.partial(settle_kernel, places),
        out_shape=jax.ShapeDtypeStruct((LAGS, 32, 128), f32),
        name="settle",
    )(sums_0, sums_1)


def body(movie, cycle_label, valid_mask):
    high, low = dft_tables()
    high, low = jnp.asarray(high), jnp.asarray(low)
    z_count = lax.axis_size("tm_1")
    z_place = lax.axis_index("tm_1")
    ends = jnp.stack([z_place == z_count - 1, z_place == 0]).astype(jnp.int32)
    labels = jnp.where(valid_mask == 1, cycle_label, -1)
    labels = lax.dynamic_slice_in_dim(labels, lax.axis_index("tm_0") * 32, 32, 1)
    labels = labels.reshape(SUB, RADIX, 8, RADIX).transpose(3, 1, 2, 0)
    to_left = [(i, (i - 1) % z_count) for i in range(z_count)]
    to_right = [(i, (i + 1) % z_count) for i in range(z_count)]
    spectra = []
    cycles = jnp.zeros((8, CYCLES), f32)

    def halo(index):
        early, late, _ = spectra[index]
        return lax.ppermute(early, "tm_1", to_left), lax.ppermute(late, "tm_1", to_right)

    def lags_of(index, beside, carry, cycles, after):
        final = index == len(CHUNKS) - 1
        early, late, _ = spectra[index]
        residues = CHUNKS[index]
        chosen = labels[residues[0]:residues[-1] + 1]
        return partial_lags(ends, early, late, *beside, chosen, cycles, carry, after, final)

    def transform_rows(index, after):
        return first_transform(movie, high, low, CHUNKS[index], after)

    def exchange(piece):
        piece = lax.all_to_all(piece.reshape((32,) + piece.shape[2:]), YROW, 0, 0, tiled=True)
        return piece.reshape((4, 8) + piece.shape[1:])

    def transform_columns(piece, index, after):
        spectra.append(second_transform(piece, high, low, len(CHUNKS[index]), after))

    piece = exchange(transform_rows(0, []))
    piece_1 = exchange(transform_rows(1, [labels]))
    transform_columns(piece, 0, [])
    halo_0 = halo(0)
    piece_2 = exchange(transform_rows(2, [spectra[0][2]]))
    transform_columns(piece_1, 1, [])
    halo_1 = halo(1)
    part_0, cycles = lags_of(0, halo_0, [], cycles, [spectra[1][2]])
    transform_columns(piece_2, 2, [cycles])
    halo_2 = halo(2)
    sums_0 = lax.all_to_all(part_0, TM, 0, 0, tiled=True)
    part_1, cycles = lags_of(1, halo_1, [], cycles, [spectra[2][2]])
    part_2, _ = lags_of(2, halo_2, [part_1], cycles, [])
    part_2, sums_0 = lax.optimization_barrier((part_2, sums_0))
    sums_1 = lax.all_to_all(part_2, TM, 0, 0, tiled=True)
    cycles = jnp.sum(sums_1[:, -1], axis=0)
    copies = jnp.broadcast_to(cycles[None], (8,) + cycles.shape)
    cycles = jnp.sum(lax.all_to_all(copies, ROW, 0, 0, tiled=True), axis=0)
    cycle_curve = cycles[:LAGS] / jnp.maximum(cycles[LAGS], 1.0)[None, :]
    return (cycle_curve, settle(sums_0, sums_1))


def solution(mesh):
    torus = Mesh(mesh.devices.reshape(4, 8, 4, 2), ("tm_0", "tm_1", "row_0", "row_1"))
    placed = (P(None, TM, ROW, None), P(None, ROW), P(None, ROW))
    return jax.shard_map(
        body, mesh=torus, in_specs=placed, out_specs=(P(), P(None, TM, ROW)), check_vma=False
    )
```

```python
import functools
import math

import jax
import jax.numpy as jnp
import ml_dtypes
import numpy as np
from jax import lax
from jax.experimental import pallas as pl
from jax.experimental.pallas import tpu as pltpu
from jax.sharding import Mesh
from jax.sharding import PartitionSpec as P

N = 1024
LAGS = 4
CYCLES = 128
FRAMES = 128
RADIX = 4
SUB = N // RADIX
OWN = 4
REST_VMEM, SECOND_VMEM, LAG_VMEM = 56, 16, 16
CHUNKS = ((0, 1), (2,), (3,))
ROW = ("row_0", "row_1")
TM = ("tm_0", "tm_1")
YROW = ("tm_0", "row_0", "row_1")

f32 = jnp.float32
bf16 = jnp.bfloat16


def dft_tables():
    freq = 4 * np.arange(SUB)[None, :, None] + np.arange(RADIX)[:, None, None]
    phase = (freq * np.arange(SUB)[None, None, :]) % N
    angle = phase * (2.0 * math.pi / N)
    table = np.concatenate([np.cos(angle), np.sin(angle)], axis=2) / 32.0
    high = table.astype(ml_dtypes.bfloat16)
    low = (table - high.astype(np.float64)).astype(ml_dtypes.bfloat16)
    return high, low


def butterfly(parts_re, parts_im, p):
    (a, b, c, d), (e, f, g, h) = parts_re, parts_im
    if p == 0:
        return (a + c) + (b + d), (e + g) + (f + h)
    if p == 2:
        return (a + c) - (b + d), (e + g) - (f + h)
    if p == 1:
        return (a - c) + (f - h), (e - g) - (b - d)
    return (a - c) - (f - h), (e - g) + (b - d)


def split(z):
    high = z.astype(bf16)
    return high, (z - high.astype(f32)).astype(bf16)


def stacked(zr, zi):
    return jnp.concatenate(
        [jnp.concatenate([zr, zi], axis=1), jnp.concatenate([zi, -zr], axis=1)], axis=0
    )


def nt(a, b):
    return lax.dot_general(a, b, (((1,), (1,)), ((), ())), preferred_element_type=f32)


def first_kernel(residues, movie_ref, high_ref, low_ref, *refs):
    out_ref = refs[-1]
    parts = [[movie_ref[c, 0, :, q * SUB:(q + 1) * SUB] for q in range(RADIX)] for c in range(2)]
    for j, p in enumerate(residues):
        zr, zi = butterfly(parts[0], parts[1], p)
        zh, zl = split(stacked(zr, zi))
        th, tl = high_ref[j], low_ref[j]
        got = nt(th, zh) + nt(tl, zh) + nt(th, zl)
        for c in range(2):
            piece = got[:, c * 128:(c + 1) * 128].reshape(8, 4, 8, 128)
            for y in range(4):
                out_ref[y, :, c, j] = piece[:, y]


def first_transform(movie, high, low, residues, after):
    count = len(residues)
    place = residues[0] // count
    table = pl.BlockSpec((count, SUB, 2 * SUB), lambda f: (place, 0, 0))
    order = [pl.BlockSpec(memory_space=pl.ANY)] * len(after)
    return pl.pallas_call(
        functools.partial(first_kernel, residues),
        grid=(OWN,),
        in_specs=[pl.BlockSpec((2, 1, 128, N), lambda f: (0, f, 0, 0)), table, table] + order,
        out_specs=pl.BlockSpec((4, 8, 2, count, 8, 128), lambda f: (0, 0, 0, 0, 0, f)),
        out_shape=jax.ShapeDtypeStruct((4, 8, 2, count, 8, OWN * 128), f32),
        compiler_params=pltpu.CompilerParams(vmem_limit_bytes=(56 if residues[0] == 0 else REST_VMEM) << 20),
        cost_estimate=pl.CostEstimate(
            flops=1024, bytes_accessed=1024, transcendentals=0
        ),
        name="first_transform",
    )(movie, high, low, *after)


def second_kernel(count, piece_ref, high_ref, low_ref, *refs):
    early_ref, late_ref, token_ref = refs[-3:]
    token_ref[...] = jnp.zeros_like(token_ref)
    for j in range(count):

        def part(c, q):
            return jnp.concatenate(
                [
                    jnp.concatenate(
                        [
                            piece_ref[y, 2 * q + h, c, j, :, f * 128:(f + 1) * 128]
                            for f in range(OWN)
                            for y in range(4)
                        ],
                        axis=0,
                    )
                    for h in range(2)
                ],
                axis=1,
            )

        parts = [[part(c, q) for q in range(RADIX)] for c in range(2)]
        for p in range(RADIX):
            zr, zi = butterfly(parts[0], parts[1], p)
            zh, zl = split(stacked(zr, zi))
            th, tl = high_ref[p], low_ref[p]
            got = nt(zh, th) + nt(zh, tl) + nt(zl, th)
            for c in range(2):
                for f in range(OWN):
                    ref = early_ref if f < 2 else late_ref
                    ref[f % 2, c, j, :, p * SUB:(p + 1) * SUB] = got[
                        (c * OWN + f) * 32:(c * OWN + f + 1) * 32
                    ]


def second_transform(piece, high, low, count, after):
    whole = (2, 2, count, 32, N)
    table = pl.BlockSpec((RADIX, SUB, 2 * SUB), lambda j: (0, 0, 0))
    out = pl.BlockSpec((2, 2, 1, 32, N), lambda j: (0, 0, j, 0, 0))
    return pl.pallas_call(
        functools.partial(second_kernel, 1),
        grid=(count,),
        in_specs=[
            pl.BlockSpec((4, 8, 2, 1, 8, OWN * 128), lambda j: (0, 0, 0, j, 0, 0)),
            table,
            table,
        ]
        + [pl.BlockSpec(memory_space=pl.ANY)] * len(after),
        out_specs=(out, out, pl.BlockSpec((8, 128), lambda j: (0, 0))),
        out_shape=(
            jax.ShapeDtypeStruct(whole, f32),
            jax.ShapeDtypeStruct(whole, f32),
            jax.ShapeDtypeStruct((8, 128), f32),
        ),
        compiler_params=pltpu.CompilerParams(vmem_limit_bytes=SECOND_VMEM << 20),
        cost_estimate=pl.CostEstimate(flops=1024, bytes_accessed=1024, transcendentals=0),
        name="second_transform",
    )(piece, high, low, *after)


def lag_kernel(
    count, carried, final, ends_ref, early_ref, late_ref, right_ref, left_ref, label_ref, before_ref,
    *refs
):
    out_ref, cycle_ref, lags_ref = refs[-3:]
    if carried:
        out_ref[:, count:count + carried] = refs[0][...]
    at_end, at_start = ends_ref[0], ends_ref[1]
    has_right = 1.0 - at_end.astype(f32)
    has_left = 1.0 - at_start.astype(f32)
    cycle_row = lax.broadcasted_iota(jnp.int32, (CYCLES, SUB), 0)
    sub_row = lax.broadcasted_iota(jnp.int32, (32, CYCLES), 0) % 8
    ones = jnp.ones((16, SUB), bf16)
    cycle_sums = jnp.zeros((32, CYCLES), f32)
    cycle_counts = jnp.zeros((16, CYCLES), f32)
    for j in range(count):
        for b in range(8):
            lanes = slice(b * 128, (b + 1) * 128)
            sums = [0.0] * LAGS
            for y in range(4):
                own_rows = slice(y * 8, (y + 1) * 8)
                right_rows = pl.ds(pl.multiple_of(8 * jnp.minimum(y + at_end, 3), 8), 8)
                left_rows = pl.ds(pl.multiple_of(8 * jnp.maximum(y - at_start, 0), 8), 8)
                frames = {}
                for f in range(2):
                    frames[f] = [early_ref[f, c, j, own_rows, lanes] for c in range(2)]
                    frames[2 + f] = [late_ref[f, c, j, own_rows, lanes] for c in range(2)]
                    frames[4 + f] = [right_ref[f, c, j, right_rows, lanes] for c in range(2)]
                    frames[f - 2] = [left_ref[f, c, j, left_rows, lanes] for c in range(2)]

                def total(pairs):
                    terms = []
                    for s, t in pairs:
                        dr = frames[t][0] - frames[s][0]
                        di = frames[t][1] - frames[s][1]
                        terms.append(dr * dr + di * di)
                    return functools.reduce(lambda x, z: x + z, terms)

                for lag in range(1, LAGS + 1):
                    own = [(s, s + lag) for s in range(OWN) if s + lag < OWN]
                    right = [(s, s + lag) for s in range(OWN) if 4 <= s + lag < 6]
                    left = [(s, s + lag) for s in (-2, -1) if s + lag in (2, 3)]
                    terms = [sums[lag - 1]]
                    if own:
                        terms.append(total(own))
                    terms.append(total(right) * has_right if y == 3 else total(right))
                    if left:
                        terms.append(total(left) * has_left if y == 0 else total(left))
                    sums[lag - 1] = functools.reduce(lambda x, z: x + z, terms)
            p, h = b // 2, b % 2
            for lag in range(1, LAGS + 1):
                lags_ref[p * 32 + (lag - 1) * 8:p * 32 + lag * 8, h * 128:(h + 1) * 128] = sums[
                    lag - 1
                ] * (1.0 / float(FRAMES - lag))
        for h in range(2):
            block = lags_ref[:, h * 128:(h + 1) * 128].T
            out_ref[16 * h:16 * h + 16, j] = block.reshape(16, 8, 128)
        for p in range(RADIX):
            dh, dl = split(lags_ref[p * 32:(p + 1) * 32, :])
            rows = jnp.concatenate([dh, dl, ones], axis=0)
            for k in range(8):
                chosen = jnp.where(cycle_row == label_ref[j, p, k:k + 1, :], 1.0, 0.0).astype(bf16)
                got = nt(rows, chosen)
                cycle_sums += jnp.where(sub_row == k, got[:32] + got[32:64], 0.0)
                cycle_counts += got[64:]
    tile = jnp.concatenate(
        [
            jnp.sum(cycle_sums.reshape(LAGS, 8, CYCLES), axis=1),
            cycle_counts[:1] * 0.125,
            jnp.zeros((3, CYCLES), f32),
        ],
        axis=0,
    ) + before_ref[...]
    cycle_ref[...] = tile
    if final:
        for m in range(32):
            out_ref[m, count + carried] = tile


def partial_lags(ends, early, late, right, left, labels, before, carry, after, final):
    count = early.shape[2]
    carried = sum(c.shape[1] for c in carry)
    vmem = pl.BlockSpec(memory_space=pltpu.VMEM)
    return pl.pallas_call(
        functools.partial(lag_kernel, count, carried, final),
        in_specs=[pl.BlockSpec(memory_space=pltpu.SMEM)]
        + [vmem] * (6 + len(carry))
        + [pl.BlockSpec(memory_space=pl.ANY)] * len(after),
        out_specs=(vmem, vmem),
        out_shape=(
            jax.ShapeDtypeStruct((32, count + carried + int(final), 8, 128), f32),
            jax.ShapeDtypeStruct((8, CYCLES), f32),
        ),
        scratch_shapes=[pltpu.VMEM((128, SUB), f32)],
        compiler_params=pltpu.CompilerParams(vmem_limit_bytes=LAG_VMEM << 20),
        cost_estimate=pl.CostEstimate(
            flops=1024, bytes_accessed=1024, transcendentals=0
        ),
        name="partial_lags",
    )(ends, early, late, right, left, labels, before, *carry, *after)


def settle_kernel(places, *refs):
    out_ref = refs[-1]
    lane = lax.broadcasted_iota(jnp.int32, (8, 128), 1)
    from_lane = (lane % 32) // 4
    tiles = []
    for y in range(4):
        for p in range(RADIX):
            which, j = places[p]
            tile = refs[which][8 * y, j]
            for z in range(1, 8):
                tile = tile + refs[which][8 * y + z, j]
            tiles.append((tile, (lane // 32 == y) & (lane % 4 == p)))
    for q in range(RADIX):
        for lag in range(LAGS):
            index = from_lane + (q * 32 + lag * 8)
            out = jnp.zeros((8, 128), f32)
            for tile, here in tiles:
                out = jnp.where(here, jnp.take_along_axis(tile, index, axis=1), out)
            out_ref[lag, pl.ds(q, 8, stride=4), :] = out


def settle(sums_0, sums_1):
    places = {}
    for j, p in enumerate(CHUNKS[0]):
        places[p] = (0, j)
    for j, p in enumerate(CHUNKS[2] + CHUNKS[1]):
        places[p] = (1, j)
    return pl.pallas_call(
        functools.partial(settle_kernel, places),
        out_shape=jax.ShapeDtypeStruct((LAGS, 32, 128), f32),
        name="settle",
    )(sums_0, sums_1)


def body(movie, cycle_label, valid_mask):
    high, low = dft_tables()
    high, low = jnp.asarray(high), jnp.asarray(low)
    z_count = lax.axis_size("tm_1")
    z_place = lax.axis_index("tm_1")
    ends = jnp.stack([z_place == z_count - 1, z_place == 0]).astype(jnp.int32)
    labels = jnp.where(valid_mask == 1, cycle_label, -1)
    labels = lax.dynamic_slice_in_dim(labels, lax.axis_index("tm_0") * 32, 32, 1)
    labels = labels.reshape(SUB, RADIX, 8, RADIX).transpose(3, 1, 2, 0)
    to_left = [(i, (i - 1) % z_count) for i in range(z_count)]
    to_right = [(i, (i + 1) % z_count) for i in range(z_count)]
    spectra = []
    cycles = jnp.zeros((8, CYCLES), f32)

    def halo(index):
        early, late, _ = spectra[index]
        return lax.ppermute(early, "tm_1", to_left), lax.ppermute(late, "tm_1", to_right)

    def lags_of(index, beside, carry, cycles, after):
        final = index == len(CHUNKS) - 1
        early, late, _ = spectra[index]
        residues = CHUNKS[index]
        chosen = labels[residues[0]:residues[-1] + 1]
        return partial_lags(ends, early, late, *beside, chosen, cycles, carry, after, final)

    def transform_rows(index, after):
        return first_transform(movie, high, low, CHUNKS[index], after)

    def exchange(piece):
        piece = lax.all_to_all(piece.reshape((32,) + piece.shape[2:]), YROW, 0, 0, tiled=True)
        return piece.reshape((4, 8) + piece.shape[1:])

    def transform_columns(piece, index, after):
        spectra.append(second_transform(piece, high, low, len(CHUNKS[index]), after))

    piece = exchange(transform_rows(0, []))
    piece_1 = exchange(transform_rows(1, [labels]))
    transform_columns(piece, 0, [])
    halo_0 = halo(0)
    piece_2 = exchange(transform_rows(2, [spectra[0][2]]))
    transform_columns(piece_1, 1, [])
    halo_1 = halo(1)
    part_0, cycles = lags_of(0, halo_0, [], cycles, [spectra[1][2]])
    transform_columns(piece_2, 2, [cycles])
    halo_2 = halo(2)
    sums_0 = lax.all_to_all(part_0, TM, 0, 0, tiled=True)
    part_1, cycles = lags_of(1, halo_1, [], cycles, [spectra[2][2]])
    part_2, _ = lags_of(2, halo_2, [part_1], cycles, [])
    part_2, sums_0 = lax.optimization_barrier((part_2, sums_0))
    sums_1 = lax.all_to_all(part_2, TM, 0, 0, tiled=True)
    cycles = jnp.sum(sums_1[:, -1], axis=0)
    copies = jnp.broadcast_to(cycles[None], (8,) + cycles.shape)
    cycles = jnp.sum(lax.all_to_all(copies, ROW, 0, 0, tiled=True), axis=0)
    cycle_curve = cycles[:LAGS] / jnp.maximum(cycles[LAGS], 1.0)[None, :]
    return (cycle_curve, settle(sums_0, sums_1))


def solution(mesh):
    torus = Mesh(mesh.devices.reshape(4, 8, 4, 2), ("tm_0", "tm_1", "row_0", "row_1"))
    placed = (P(None, TM, ROW, None), P(None, ROW), P(None, ROW))
    return jax.shard_map(
        body, mesh=torus, in_specs=placed, out_specs=(P(), P(None, TM, ROW)), check_vma=False
    )
```

```python
import functools
import math

import jax
import jax.numpy as jnp
import ml_dtypes
import numpy as np
from jax import lax
from jax.experimental import pallas as pl
from jax.experimental.pallas import tpu as pltpu
from jax.sharding import Mesh
from jax.sharding import PartitionSpec as P

N = 1024
LAGS = 4
CYCLES = 128
FRAMES = 128
RADIX = 4
SUB = N // RADIX
OWN = 4
REST_VMEM, SECOND_VMEM, LAG_VMEM = 56, 16, 16
CHUNKS = ((0, 1), (2,), (3,))
ROW = ("row_0", "row_1")
TM = ("tm_0", "tm_1")
ROWY = ("row_0", "row_1", "tm_0")

f32 = jnp.float32
bf16 = jnp.bfloat16


def dft_tables():
    freq = 4 * np.arange(SUB)[None, :, None] + np.arange(RADIX)[:, None, None]
    phase = (freq * np.arange(SUB)[None, None, :]) % N
    angle = phase * (2.0 * math.pi / N)
    table = np.concatenate([np.cos(angle), np.sin(angle)], axis=2) / 32.0
    high = table.astype(ml_dtypes.bfloat16)
    low = (table - high.astype(np.float64)).astype(ml_dtypes.bfloat16)
    return high, low


def butterfly(parts_re, parts_im, p):
    (a, b, c, d), (e, f, g, h) = parts_re, parts_im
    if p == 0:
        return (a + c) + (b + d), (e + g) + (f + h)
    if p == 2:
        return (a + c) - (b + d), (e + g) - (f + h)
    if p == 1:
        return (a - c) + (f - h), (e - g) - (b - d)
    return (a - c) - (f - h), (e - g) + (b - d)


def split(z):
    high = z.astype(bf16)
    return high, (z - high.astype(f32)).astype(bf16)


def stacked(zr, zi):
    return jnp.concatenate(
        [jnp.concatenate([zr, zi], axis=1), jnp.concatenate([zi, -zr], axis=1)], axis=0
    )


def nt(a, b):
    return lax.dot_general(a, b, (((1,), (1,)), ((), ())), preferred_element_type=f32)


def first_kernel(residues, movie_ref, high_ref, low_ref, *refs):
    out_ref = refs[-1]
    parts = [[movie_ref[c, 0, :, q * SUB:(q + 1) * SUB] for q in range(RADIX)] for c in range(2)]
    for j, p in enumerate(residues):
        zr, zi = butterfly(parts[0], parts[1], p)
        zh, zl = split(stacked(zr, zi))
        th, tl = high_ref[j], low_ref[j]
        got = nt(th, zh) + nt(tl, zh) + nt(th, zl)
        for c in range(2):
            out_ref[:, :, c, j] = got[:, c * 128:(c + 1) * 128].reshape(8, 4, 8, 128)


def first_transform(movie, high, low, residues, after):
    count = len(residues)
    place = residues[0] // count
    table = pl.BlockSpec((count, SUB, 2 * SUB), lambda f: (place, 0, 0))
    order = [pl.BlockSpec(memory_space=pl.ANY)] * len(after)
    return pl.pallas_call(
        functools.partial(first_kernel, residues),
        grid=(OWN,),
        in_specs=[pl.BlockSpec((2, 1, 128, N), lambda f: (0, f, 0, 0)), table, table] + order,
        out_specs=pl.BlockSpec((8, 4, 2, count, 8, 128), lambda f: (0, 0, 0, 0, 0, f)),
        out_shape=jax.ShapeDtypeStruct((8, 4, 2, count, 8, OWN * 128), f32),
        compiler_params=pltpu.CompilerParams(vmem_limit_bytes=(56 if residues[0] == 0 else REST_VMEM) << 20),
        cost_estimate=pl.CostEstimate(
            flops=1024, bytes_accessed=1024, transcendentals=0
        ),
        name="first_transform",
    )(movie, high, low, *after)


def second_kernel(count, piece_ref, high_ref, low_ref, *refs):
    early_ref, late_ref, token_ref = refs[-3:]
    token_ref[...] = jnp.zeros_like(token_ref)
    for j in range(count):

        def part(c, q):
            return jnp.concatenate(
                [
                    jnp.concatenate(
                        [
                            piece_ref[2 * q + h, y, c, j, :, f * 128:(f + 1) * 128]
                            for f in range(OWN)
                            for y in range(4)
                        ],
                        axis=0,
                    )
                    for h in range(2)
                ],
                axis=1,
            )

        parts = [[part(c, q) for q in range(RADIX)] for c in range(2)]
        for p in range(RADIX):
            zr, zi = butterfly(parts[0], parts[1], p)
            zh, zl = split(stacked(zr, zi))
            th, tl = high_ref[p], low_ref[p]
            got = nt(zh, th) + nt(zh, tl) + nt(zl, th)
            for c in range(2):
                for f in range(OWN):
                    ref = early_ref if f < 2 else late_ref
                    ref[f % 2, c, j, :, p * SUB:(p + 1) * SUB] = got[
                        (c * OWN + f) * 32:(c * OWN + f + 1) * 32
                    ]


def second_transform(piece, high, low, count, after):
    whole = (2, 2, count, 32, N)
    table = pl.BlockSpec((RADIX, SUB, 2 * SUB), lambda j: (0, 0, 0))
    out = pl.BlockSpec((2, 2, 1, 32, N), lambda j: (0, 0, j, 0, 0))
    return pl.pallas_call(
        functools.partial(second_kernel, 1),
        grid=(count,),
        in_specs=[
            pl.BlockSpec((8, 4, 2, 1, 8, OWN * 128), lambda j: (0, 0, 0, j, 0, 0)),
            table,
            table,
        ]
        + [pl.BlockSpec(memory_space=pl.ANY)] * len(after),
        out_specs=(out, out, pl.BlockSpec((8, 128), lambda j: (0, 0))),
        out_shape=(
            jax.ShapeDtypeStruct(whole, f32),
            jax.ShapeDtypeStruct(whole, f32),
            jax.ShapeDtypeStruct((8, 128), f32),
        ),
        compiler_params=pltpu.CompilerParams(vmem_limit_bytes=SECOND_VMEM << 20),
        cost_estimate=pl.CostEstimate(flops=1024, bytes_accessed=1024, transcendentals=0),
        name="second_transform",
    )(piece, high, low, *after)


def lag_kernel(
    count, carried, final, ends_ref, early_ref, late_ref, right_ref, left_ref, label_ref, before_ref,
    *refs
):
    out_ref, cycle_ref, lags_ref = refs[-3:]
    if carried:
        out_ref[:, count:count + carried] = refs[0][...]
    at_end, at_start = ends_ref[0], ends_ref[1]
    has_right = 1.0 - at_end.astype(f32)
    has_left = 1.0 - at_start.astype(f32)
    cycle_row = lax.broadcasted_iota(jnp.int32, (CYCLES, SUB), 0)
    sub_row = lax.broadcasted_iota(jnp.int32, (32, CYCLES), 0) % 8
    ones = jnp.ones((16, SUB), bf16)
    cycle_sums = jnp.zeros((32, CYCLES), f32)
    cycle_counts = jnp.zeros((16, CYCLES), f32)
    for j in range(count):
        for b in range(8):
            lanes = slice(b * 128, (b + 1) * 128)
            sums = [0.0] * LAGS
            for y in range(4):
                own_rows = slice(y * 8, (y + 1) * 8)
                right_rows = pl.ds(pl.multiple_of(8 * jnp.minimum(y + at_end, 3), 8), 8)
                left_rows = pl.ds(pl.multiple_of(8 * jnp.maximum(y - at_start, 0), 8), 8)
                frames = {}
                for f in range(2):
                    frames[f] = [early_ref[f, c, j, own_rows, lanes] for c in range(2)]
                    frames[2 + f] = [late_ref[f, c, j, own_rows, lanes] for c in range(2)]
                    frames[4 + f] = [right_ref[f, c, j, right_rows, lanes] for c in range(2)]
                    frames[f - 2] = [left_ref[f, c, j, left_rows, lanes] for c in range(2)]

                def total(pairs):
                    terms = []
                    for s, t in pairs:
                        dr = frames[t][0] - frames[s][0]
                        di = frames[t][1] - frames[s][1]
                        terms.append(dr * dr + di * di)
                    return functools.reduce(lambda x, z: x + z, terms)

                for lag in range(1, LAGS + 1):
                    own = [(s, s + lag) for s in range(OWN) if s + lag < OWN]
                    right = [(s, s + lag) for s in range(OWN) if 4 <= s + lag < 6]
                    left = [(s, s + lag) for s in (-2, -1) if s + lag in (2, 3)]
                    terms = [sums[lag - 1]]
                    if own:
                        terms.append(total(own))
                    terms.append(total(right) * has_right if y == 3 else total(right))
                    if left:
                        terms.append(total(left) * has_left if y == 0 else total(left))
                    sums[lag - 1] = functools.reduce(lambda x, z: x + z, terms)
            p, h = b // 2, b % 2
            for lag in range(1, LAGS + 1):
                lags_ref[p * 32 + (lag - 1) * 8:p * 32 + lag * 8, h * 128:(h + 1) * 128] = sums[
                    lag - 1
                ] * (1.0 / float(FRAMES - lag))
        for h in range(2):
            block = lags_ref[:, h * 128:(h + 1) * 128].T
            out_ref[16 * h:16 * h + 16, j] = block.reshape(16, 8, 128)
        for p in range(RADIX):
            dh, dl = split(lags_ref[p * 32:(p + 1) * 32, :])
            rows = jnp.concatenate([dh, dl, ones], axis=0)
            for k in range(8):
                chosen = jnp.where(cycle_row == label_ref[j, p, k:k + 1, :], 1.0, 0.0).astype(bf16)
                got = nt(rows, chosen)
                cycle_sums += jnp.where(sub_row == k, got[:32] + got[32:64], 0.0)
                cycle_counts += got[64:]
    tile = jnp.concatenate(
        [
            jnp.sum(cycle_sums.reshape(LAGS, 8, CYCLES), axis=1),
            cycle_counts[:1] * 0.125,
            jnp.zeros((3, CYCLES), f32),
        ],
        axis=0,
    ) + before_ref[...]
    cycle_ref[...] = tile
    if final:
        for m in range(32):
            out_ref[m, count + carried] = tile


def partial_lags(ends, early, late, right, left, labels, before, carry, after, final):
    count = early.shape[2]
    carried = sum(c.shape[1] for c in carry)
    vmem = pl.BlockSpec(memory_space=pltpu.VMEM)
    return pl.pallas_call(
        functools.partial(lag_kernel, count, carried, final),
        in_specs=[pl.BlockSpec(memory_space=pltpu.SMEM)]
        + [vmem] * (6 + len(carry))
        + [pl.BlockSpec(memory_space=pl.ANY)] * len(after),
        out_specs=(vmem, vmem),
        out_shape=(
            jax.ShapeDtypeStruct((32, count + carried + int(final), 8, 128), f32),
            jax.ShapeDtypeStruct((8, CYCLES), f32),
        ),
        scratch_shapes=[pltpu.VMEM((128, SUB), f32)],
        compiler_params=pltpu.CompilerParams(vmem_limit_bytes=LAG_VMEM << 20),
        cost_estimate=pl.CostEstimate(
            flops=1024, bytes_accessed=1024, transcendentals=0
        ),
        name="partial_lags",
    )(ends, early, late, right, left, labels, before, *carry, *after)


def settle_kernel(places, *refs):
    out_ref = refs[-1]
    lane = lax.broadcasted_iota(jnp.int32, (8, 128), 1)
    from_lane = (lane % 32) // 4
    tiles = []
    for y in range(4):
        for p in range(RADIX):
            which, j = places[p]
            tile = refs[which][8 * y, j]
            for z in range(1, 8):
                tile = tile + refs[which][8 * y + z, j]
            tiles.append((tile, (lane // 32 == y) & (lane % 4 == p)))
    for q in range(RADIX):
        for lag in range(LAGS):
            index = from_lane + (q * 32 + lag * 8)
            out = jnp.zeros((8, 128), f32)
            for tile, here in tiles:
                out = jnp.where(here, jnp.take_along_axis(tile, index, axis=1), out)
            out_ref[lag, pl.ds(q, 8, stride=4), :] = out


def settle(sums_0, sums_1):
    places = {}
    for j, p in enumerate(CHUNKS[0]):
        places[p] = (0, j)
    for j, p in enumerate(CHUNKS[2] + CHUNKS[1]):
        places[p] = (1, j)
    return pl.pallas_call(
        functools.partial(settle_kernel, places),
        out_shape=jax.ShapeDtypeStruct((LAGS, 32, 128), f32),
        name="settle",
    )(sums_0, sums_1)


def body(movie, cycle_label, valid_mask):
    high, low = dft_tables()
    high, low = jnp.asarray(high), jnp.asarray(low)
    z_count = lax.axis_size("tm_1")
    z_place = lax.axis_index("tm_1")
    ends = jnp.stack([z_place == z_count - 1, z_place == 0]).astype(jnp.int32)
    labels = jnp.where(valid_mask == 1, cycle_label, -1)
    labels = lax.dynamic_slice_in_dim(labels, lax.axis_index("tm_0") * 32, 32, 1)
    labels = labels.reshape(SUB, RADIX, 8, RADIX).transpose(3, 1, 2, 0)
    to_left = [(i, (i - 1) % z_count) for i in range(z_count)]
    to_right = [(i, (i + 1) % z_count) for i in range(z_count)]
    spectra = []
    cycles = jnp.zeros((8, CYCLES), f32)

    def halo(index):
        early, late, _ = spectra[index]
        return lax.ppermute(early, "tm_1", to_left), lax.ppermute(late, "tm_1", to_right)

    def lags_of(index, beside, carry, cycles, after):
        final = index == len(CHUNKS) - 1
        early, late, _ = spectra[index]
        residues = CHUNKS[index]
        chosen = labels[residues[0]:residues[-1] + 1]
        return partial_lags(ends, early, late, *beside, chosen, cycles, carry, after, final)

    def transform_rows(index, after):
        return first_transform(movie, high, low, CHUNKS[index], after)

    def exchange(piece):
        piece = lax.all_to_all(piece.reshape((32,) + piece.shape[2:]), ROWY, 0, 0, tiled=True)
        return piece.reshape((8, 4) + piece.shape[1:])

    def transform_columns(piece, index, after):
        spectra.append(second_transform(piece, high, low, len(CHUNKS[index]), after))

    piece = exchange(transform_rows(0, []))
    piece_1 = exchange(transform_rows(1, [labels]))
    transform_columns(piece, 0, [])
    halo_0 = halo(0)
    piece_2 = exchange(transform_rows(2, [spectra[0][2]]))
    transform_columns(piece_1, 1, [])
    halo_1 = halo(1)
    part_0, cycles = lags_of(0, halo_0, [], cycles, [spectra[1][2]])
    transform_columns(piece_2, 2, [cycles])
    halo_2 = halo(2)
    sums_0 = lax.all_to_all(part_0, TM, 0, 0, tiled=True)
    part_1, cycles = lags_of(1, halo_1, [], cycles, [spectra[2][2]])
    part_2, _ = lags_of(2, halo_2, [part_1], cycles, [])
    part_2, sums_0 = lax.optimization_barrier((part_2, sums_0))
    sums_1 = lax.all_to_all(part_2, TM, 0, 0, tiled=True)
    cycles = jnp.sum(sums_1[:, -1], axis=0)
    copies = jnp.broadcast_to(cycles[None], (8,) + cycles.shape)
    cycles = jnp.sum(lax.all_to_all(copies, ROW, 0, 0, tiled=True), axis=0)
    cycle_curve = cycles[:LAGS] / jnp.maximum(cycles[LAGS], 1.0)[None, :]
    return (cycle_curve, settle(sums_0, sums_1))


def solution(mesh):
    torus = Mesh(mesh.devices.reshape(4, 8, 4, 2), ("tm_0", "tm_1", "row_0", "row_1"))
    placed = (P(None, TM, ROW, None), P(None, ROW), P(None, ROW))
    return jax.shard_map(
        body, mesh=torus, in_specs=placed, out_specs=(P(), P(None, TM, ROW)), check_vma=False
    )
```

```python
import functools
import math

import jax
import jax.numpy as jnp
import ml_dtypes
import numpy as np
from jax import lax
from jax.experimental import pallas as pl
from jax.experimental.pallas import tpu as pltpu
from jax.sharding import Mesh
from jax.sharding import PartitionSpec as P

N = 1024
LAGS = 4
CYCLES = 128
FRAMES = 128
RADIX = 4
SUB = N // RADIX
OWN = 4
REST_VMEM, SECOND_VMEM, LAG_VMEM = 56, 16, 16
CHUNKS = ((0, 1), (2,), (3,))
ROW = ("row_0", "row_1")
TM = ("tm_0", "tm_1")
ROWY = ("row_0", "row_1", "tm_0")

f32 = jnp.float32
bf16 = jnp.bfloat16


def dft_tables():
    freq = 4 * np.arange(SUB)[None, :, None] + np.arange(RADIX)[:, None, None]
    phase = (freq * np.arange(SUB)[None, None, :]) % N
    angle = phase * (2.0 * math.pi / N)
    table = np.concatenate([np.cos(angle), np.sin(angle)], axis=2) / 32.0
    high = table.astype(ml_dtypes.bfloat16)
    low = (table - high.astype(np.float64)).astype(ml_dtypes.bfloat16)
    return high, low


def butterfly(parts_re, parts_im, p):
    (a, b, c, d), (e, f, g, h) = parts_re, parts_im
    if p == 0:
        return (a + c) + (b + d), (e + g) + (f + h)
    if p == 2:
        return (a + c) - (b + d), (e + g) - (f + h)
    if p == 1:
        return (a - c) + (f - h), (e - g) - (b - d)
    return (a - c) - (f - h), (e - g) + (b - d)


def split(z):
    high = z.astype(bf16)
    return high, (z - high.astype(f32)).astype(bf16)


def stacked(zr, zi):
    return jnp.concatenate(
        [jnp.concatenate([zr, zi], axis=1), jnp.concatenate([zi, -zr], axis=1)], axis=0
    )


def nt(a, b):
    return lax.dot_general(a, b, (((1,), (1,)), ((), ())), preferred_element_type=f32)


def first_kernel(residues, movie_ref, high_ref, low_ref, *refs):
    out_ref = refs[-1]
    parts = [[movie_ref[c, 0, :, q * SUB:(q + 1) * SUB] for q in range(RADIX)] for c in range(2)]
    for j, p in enumerate(residues):
        zr, zi = butterfly(parts[0], parts[1], p)
        zh, zl = split(stacked(zr, zi))
        th, tl = high_ref[j], low_ref[j]
        got = nt(th, zh) + nt(tl, zh) + nt(th, zl)
        for c in range(2):
            out_ref[:, :, c, j] = got[:, c * 128:(c + 1) * 128].reshape(8, 4, 8, 128)


def first_transform(movie, high, low, residues, after):
    count = len(residues)
    place = residues[0] // count
    table = pl.BlockSpec((count, SUB, 2 * SUB), lambda f: (place, 0, 0))
    order = [pl.BlockSpec(memory_space=pl.ANY)] * len(after)
    return pl.pallas_call(
        functools.partial(first_kernel, residues),
        grid=(OWN,),
        in_specs=[pl.BlockSpec((2, 1, 128, N), lambda f: (0, f, 0, 0)), table, table] + order,
        out_specs=pl.BlockSpec((8, 4, 2, count, 8, 128), lambda f: (0, 0, 0, 0, 0, f)),
        out_shape=jax.ShapeDtypeStruct((8, 4, 2, count, 8, OWN * 128), f32),
        compiler_params=pltpu.CompilerParams(vmem_limit_bytes=(56 if residues[0] == 0 else REST_VMEM) << 20),
        cost_estimate=pl.CostEstimate(
            flops=1024, bytes_accessed=1024, transcendentals=0
        ),
        name="first_transform",
    )(movie, high, low, *after)


def second_kernel(count, piece_ref, high_ref, low_ref, *refs):
    early_ref, late_ref, token_ref = refs[-3:]
    token_ref[...] = jnp.zeros_like(token_ref)
    for j in range(count):

        def part(c, q):
            return jnp.concatenate(
                [
                    jnp.concatenate(
                        [
                            piece_ref[2 * q + h, y, c, j, :, f * 128:(f + 1) * 128]
                            for f in range(OWN)
                            for y in range(4)
                        ],
                        axis=0,
                    )
                    for h in range(2)
                ],
                axis=1,
            )

        parts = [[part(c, q) for q in range(RADIX)] for c in range(2)]
        for p in range(RADIX):
            zr, zi = butterfly(parts[0], parts[1], p)
            zh, zl = split(stacked(zr, zi))
            th, tl = high_ref[p], low_ref[p]
            got = nt(zh, th) + nt(zh, tl) + nt(zl, th)
            for c in range(2):
                for f in range(OWN):
                    ref = early_ref if f < 2 else late_ref
                    ref[f % 2, c, j, :, p * SUB:(p + 1) * SUB] = got[
                        (c * OWN + f) * 32:(c * OWN + f + 1) * 32
                    ]


def second_transform(piece, high, low, count, after):
    vmem = pl.BlockSpec(memory_space=pltpu.VMEM)
    half = jax.ShapeDtypeStruct((2, 2, count, 32, N), f32)
    return pl.pallas_call(
        functools.partial(second_kernel, count),
        in_specs=[vmem] * 3 + [pl.BlockSpec(memory_space=pl.ANY)] * len(after),
        out_shape=(half, half, jax.ShapeDtypeStruct((8, 128), f32)),
        compiler_params=pltpu.CompilerParams(vmem_limit_bytes=SECOND_VMEM << 20),
        cost_estimate=pl.CostEstimate(
            flops=1024, bytes_accessed=1024, transcendentals=0
        ),
        name="second_transform",
    )(piece, high, low, *after)


def lag_kernel(
    count, carried, final, ends_ref, early_ref, late_ref, right_ref, left_ref, label_ref, before_ref,
    *refs
):
    out_ref, cycle_ref, lags_ref = refs[-3:]
    if carried:
        out_ref[:, count:count + carried] = refs[0][...]
    at_end, at_start = ends_ref[0], ends_ref[1]
    has_right = 1.0 - at_end.astype(f32)
    has_left = 1.0 - at_start.astype(f32)
    cycle_row = lax.broadcasted_iota(jnp.int32, (CYCLES, SUB), 0)
    sub_row = lax.broadcasted_iota(jnp.int32, (32, CYCLES), 0) % 8
    ones = jnp.ones((16, SUB), bf16)
    cycle_sums = jnp.zeros((32, CYCLES), f32)
    cycle_counts = jnp.zeros((16, CYCLES), f32)
    def lag_block(step, _):
        j, b = step // 8, step % 8
        p, h = b // 2, b % 2
        lanes = pl.ds(pl.multiple_of(b * 128, 128), 128)
        sums = [0.0] * LAGS
        for y in range(4):
            own_rows = slice(y * 8, (y + 1) * 8)
            right_rows = pl.ds(pl.multiple_of(8 * jnp.minimum(y + at_end, 3), 8), 8)
            left_rows = pl.ds(pl.multiple_of(8 * jnp.maximum(y - at_start, 0), 8), 8)
            frames = {}
            for f in range(2):
                frames[f] = [early_ref[f, c, j, own_rows, lanes] for c in range(2)]
                frames[2 + f] = [late_ref[f, c, j, own_rows, lanes] for c in range(2)]
                frames[4 + f] = [right_ref[f, c, j, right_rows, lanes] for c in range(2)]
                frames[f - 2] = [left_ref[f, c, j, left_rows, lanes] for c in range(2)]

            def total(pairs):
                terms = []
                for s, t in pairs:
                    dr = frames[t][0] - frames[s][0]
                    di = frames[t][1] - frames[s][1]
                    terms.append(dr * dr + di * di)
                return functools.reduce(lambda x, z: x + z, terms)

            for lag in range(1, LAGS + 1):
                own = [(s, s + lag) for s in range(OWN) if s + lag < OWN]
                right = [(s, s + lag) for s in range(OWN) if 4 <= s + lag < 6]
                left = [(s, s + lag) for s in (-2, -1) if s + lag in (2, 3)]
                terms = [sums[lag - 1]]
                if own:
                    terms.append(total(own))
                terms.append(total(right) * has_right if y == 3 else total(right))
                if left:
                    terms.append(total(left) * has_left if y == 0 else total(left))
                sums[lag - 1] = functools.reduce(lambda x, z: x + z, terms)
        place = pl.multiple_of(j * 128 + p * 32, 32)
        stacked_lags = jnp.concatenate(
            [sums[lag - 1] * (1.0 / float(FRAMES - lag)) for lag in range(1, LAGS + 1)], axis=0
        )
        lags_ref[h, pl.ds(place, 32), :] = stacked_lags
        return 0

    lax.fori_loop(0, 8 * count, lag_block, 0)
    for j in range(count):
        for h in range(2):
            block = lags_ref[h, j * 128:(j + 1) * 128, :].T
            out_ref[16 * h:16 * h + 16, j] = block.reshape(16, 8, 128)

    def cycle_block(step, carried_sums):
        cycle_sums, cycle_counts = carried_sums
        place = pl.ds(pl.multiple_of(step * 32, 32), 32)
        dh, dl = split(jnp.concatenate([lags_ref[h, place, :] for h in range(2)], axis=1))
        rows = jnp.concatenate([dh, dl, ones], axis=0)
        for k in range(8):
            label_row = label_ref[step // RADIX, step % RADIX, k:k + 1, :]
            chosen = jnp.where(cycle_row == label_row, 1.0, 0.0).astype(bf16)
            got = nt(rows, chosen)
            cycle_sums += jnp.where(sub_row == k, got[:32] + got[32:64], 0.0)
            cycle_counts += got[64:]
        return cycle_sums, cycle_counts

    cycle_sums, cycle_counts = lax.fori_loop(
        0, RADIX * count, cycle_block, (cycle_sums, cycle_counts)
    )
    tile = jnp.concatenate(
        [
            jnp.sum(cycle_sums.reshape(LAGS, 8, CYCLES), axis=1),
            cycle_counts[:1] * 0.125,
            jnp.zeros((3, CYCLES), f32),
        ],
        axis=0,
    ) + before_ref[...]
    cycle_ref[...] = tile
    if final:
        for m in range(32):
            out_ref[m, count + carried] = tile


def partial_lags(ends, early, late, right, left, labels, before, carry, after, final):
    count = early.shape[2]
    carried = sum(c.shape[1] for c in carry)
    vmem = pl.BlockSpec(memory_space=pltpu.VMEM)
    return pl.pallas_call(
        functools.partial(lag_kernel, count, carried, final),
        in_specs=[pl.BlockSpec(memory_space=pltpu.SMEM)]
        + [vmem] * (6 + len(carry))
        + [pl.BlockSpec(memory_space=pl.ANY)] * len(after),
        out_specs=(vmem, vmem),
        out_shape=(
            jax.ShapeDtypeStruct((32, count + carried + int(final), 8, 128), f32),
            jax.ShapeDtypeStruct((8, CYCLES), f32),
        ),
        scratch_shapes=[pltpu.VMEM((2, 128 * count, 128), f32)],
        compiler_params=pltpu.CompilerParams(vmem_limit_bytes=LAG_VMEM << 20),
        cost_estimate=pl.CostEstimate(
            flops=1024, bytes_accessed=1024, transcendentals=0
        ),
        name="partial_lags",
    )(ends, early, late, right, left, labels, before, *carry, *after)


def settle_kernel(places, *refs):
    out_ref = refs[-1]
    lane = lax.broadcasted_iota(jnp.int32, (8, 128), 1)
    from_lane = (lane % 32) // 4
    tiles = []
    for y in range(4):
        for p in range(RADIX):
            which, j = places[p]
            tile = refs[which][8 * y, j]
            for z in range(1, 8):
                tile = tile + refs[which][8 * y + z, j]
            tiles.append((tile, (lane // 32 == y) & (lane % 4 == p)))
    for q in range(RADIX):
        for lag in range(LAGS):
            index = from_lane + (q * 32 + lag * 8)
            out = jnp.zeros((8, 128), f32)
            for tile, here in tiles:
                out = jnp.where(here, jnp.take_along_axis(tile, index, axis=1), out)
            out_ref[lag, pl.ds(q, 8, stride=4), :] = out


def settle(sums_0, sums_1):
    places = {}
    for j, p in enumerate(CHUNKS[0]):
        places[p] = (0, j)
    for j, p in enumerate(CHUNKS[2] + CHUNKS[1]):
        places[p] = (1, j)
    return pl.pallas_call(
        functools.partial(settle_kernel, places),
        out_shape=jax.ShapeDtypeStruct((LAGS, 32, 128), f32),
        name="settle",
    )(sums_0, sums_1)


def body(movie, cycle_label, valid_mask):
    high, low = dft_tables()
    high, low = jnp.asarray(high), jnp.asarray(low)
    z_count = lax.axis_size("tm_1")
    z_place = lax.axis_index("tm_1")
    ends = jnp.stack([z_place == z_count - 1, z_place == 0]).astype(jnp.int32)
    labels = jnp.where(valid_mask == 1, cycle_label, -1)
    labels = lax.dynamic_slice_in_dim(labels, lax.axis_index("tm_0") * 32, 32, 1)
    labels = labels.reshape(SUB, RADIX, 8, RADIX).transpose(3, 1, 2, 0)
    to_left = [(i, (i - 1) % z_count) for i in range(z_count)]
    to_right = [(i, (i + 1) % z_count) for i in range(z_count)]
    spectra = []
    cycles = jnp.zeros((8, CYCLES), f32)

    def halo(index):
        early, late, _ = spectra[index]
        return lax.ppermute(early, "tm_1", to_left), lax.ppermute(late, "tm_1", to_right)

    def lags_of(index, beside, carry, cycles, after):
        final = index == len(CHUNKS) - 1
        early, late, _ = spectra[index]
        residues = CHUNKS[index]
        chosen = labels[residues[0]:residues[-1] + 1]
        return partial_lags(ends, early, late, *beside, chosen, cycles, carry, after, final)

    def transform_rows(index, after):
        return first_transform(movie, high, low, CHUNKS[index], after)

    def exchange(piece):
        piece = lax.all_to_all(piece.reshape((32,) + piece.shape[2:]), ROWY, 0, 0, tiled=True)
        return piece.reshape((8, 4) + piece.shape[1:])

    def transform_columns(piece, index, after):
        spectra.append(second_transform(piece, high, low, len(CHUNKS[index]), after))

    piece = exchange(transform_rows(0, []))
    piece_1 = exchange(transform_rows(1, [labels]))
    transform_columns(piece, 0, [])
    halo_0 = halo(0)
    piece_2 = exchange(transform_rows(2, [spectra[0][2]]))
    transform_columns(piece_1, 1, [])
    halo_1 = halo(1)
    part_0, cycles = lags_of(0, halo_0, [], cycles, [spectra[1][2]])
    transform_columns(piece_2, 2, [cycles])
    halo_2 = halo(2)
    sums_0 = lax.all_to_all(part_0, TM, 0, 0, tiled=True)
    part_1, cycles = lags_of(1, halo_1, [], cycles, [spectra[2][2]])
    part_2, _ = lags_of(2, halo_2, [part_1], cycles, [])
    part_2, sums_0 = lax.optimization_barrier((part_2, sums_0))
    sums_1 = lax.all_to_all(part_2, TM, 0, 0, tiled=True)
    cycles = jnp.sum(sums_1[:, -1], axis=0)
    copies = jnp.broadcast_to(cycles[None], (8,) + cycles.shape)
    cycles = jnp.sum(lax.all_to_all(copies, ROW, 0, 0, tiled=True), axis=0)
    cycle_curve = cycles[:LAGS] / jnp.maximum(cycles[LAGS], 1.0)[None, :]
    return (cycle_curve, settle(sums_0, sums_1))


def solution(mesh):
    torus = Mesh(mesh.devices.reshape(4, 8, 4, 2), ("tm_0", "tm_1", "row_0", "row_1"))
    placed = (P(None, TM, ROW, None), P(None, ROW), P(None, ROW))
    return jax.shard_map(
        body, mesh=torus, in_specs=placed, out_specs=(P(), P(None, TM, ROW)), check_vma=False
    )
```
